32 devices in a mesh: prow: 4 (over x, core), pcol: 8 (over z, y).
Axes of the slice: x: 2, y: 2, z: 4, core: 2. Of those that a mesh axis runs over, the one named last changes fastest.
Arguments:
- diag_block: float32 [640, 640], P('prow'), as said below
- panel_below: float32 [18432, 640], P(('prow', 'pcol')), may hold values from -0.5 to 0.5
- trailing: float32 [18432, 18432], P('prow', 'pcol'), may hold values from -6 to 6
Outputs:
- factor_diag: float32 [640, 640], P('prow')
- factor_below: float32 [18432, 640], P(('prow', 'pcol'))
- updated: float32 [18432, 18432], P('prow', 'pcol')
The draws below stay inside these ranges and needn't reach their ends.
Inputs may be any that keep to these rules, and one draw needn't show every extreme that they name: `diag_block`: symmetric and positive definite, its smallest eigenvalue above 0.5.
All inputs are finite; a program needn't handle non-finite values.
Results may differ from the reference program's by a relative error of at most 0.0003.
Values sent between devices are 32-bit elements; how exact they have to be, the bound alone decides.
A program may use at most 192 MiB of HBM per device.

```python
import jax
import jax.numpy as jnp
from jax import lax

M = 18432
P_SIZE = 640


def draw_diag_block(key, part):
    east_key = jax.random.fold_in(key, 11)
    north_key = jax.random.fold_in(key, 23)
    nugget_key = jax.random.fold_in(key, 37)
    length_scale = 1.265 / P_SIZE ** 0.5
    variance = 20.0
    nugget = jax.random.uniform(nugget_key, (P_SIZE,), jnp.float32, 0.6, 1.2)
    eastings = jax.random.uniform(east_key, (P_SIZE,), jnp.float32, 0.0, 1.0)
    northings = jax.random.uniform(north_key, (P_SIZE,), jnp.float32, 0.0, 1.0)
    east_gap = eastings[:, None] - eastings[None, :]
    north_gap = northings[:, None] - northings[None, :]
    distance = jnp.sqrt(east_gap * east_gap + north_gap * north_gap)
    scaled = distance * (3.0 ** 0.5 / length_scale)
    kernel = variance * (1.0 + scaled) * jnp.exp(-scaled)
    return kernel + jnp.diag(nugget)


def steps_of(key, dims, pieces, least, top_value):
    def one(position, blocks):
        heights = jax.random.uniform(jax.random.fold_in(jax.random.fold_in(key, 6), position), (blocks,), jnp.float32, least / len(pieces), top_value / len(pieces))
        return jnp.repeat(jnp.exp(heights), dims[position] // blocks).reshape((-1,) + (1,) * (len(dims) - position - 1))

    loudness = one(*pieces[0])
    for cut in pieces[1:]:
        loudness = loudness * one(*cut)
    return loudness


def bell_draw(stream_key, extent, width, limit, pieces=(), dtype=jnp.bfloat16):
    factor_of = steps_of(stream_key, extent, pieces, -0.22, 0.18) if pieces else 1.0
    result = jax.random.normal(stream_key, extent, jnp.float32) * width * factor_of
    return jnp.minimum(jnp.maximum(result, -limit), limit).astype(dtype)


def setup_inputs(seed: int = 0) -> dict:
    key_of = jax.random.split(jax.random.key(seed), 4)
    return {
        "diag_block": draw_diag_block(jax.random.fold_in(key_of[3], 71), 0),
        "panel_below": bell_draw(key_of[1], (M, P_SIZE), (P_SIZE // 4) ** -0.5, 0.5, ((0, 32),), jnp.float32),
        "trailing": bell_draw(key_of[2], (M, M), 1.0, 6.0, ((0, 4), (1, 8)), jnp.float32),
    }


def reference(diag_block, panel_below, trailing):
    factor_diag = jnp.linalg.cholesky(diag_block)
    factor_below = jax.scipy.linalg.solve_triangular(factor_diag, panel_below.T, lower=True).T
    product = lax.dot_general(factor_below.astype(jnp.float32), factor_below.astype(jnp.float32), (((1,), (1,)), ((), ())), precision=lax.Precision.HIGHEST, preferred_element_type=jnp.float32)
    updated = trailing - product
    return (factor_diag, factor_below, updated)
```

```python
import functools

import jax
import jax.numpy as jnp
import numpy as np
from jax import lax
from jax.experimental import pallas as pl
from jax.experimental.pallas import tpu as pltpu
from jax.sharding import PartitionSpec as P

B = 128
F32 = jnp.float32
BF16 = jnp.bfloat16
VMEM = pl.BlockSpec(memory_space=pltpu.VMEM)


def dot(a, b, contract=((1,), (0,)), precision=lax.Precision.HIGHEST):
    return lax.dot_general(a, b, (contract, ((), ())), precision=precision, preferred_element_type=F32)


def split(x):
    high = x.astype(BF16)
    return high, (x - high.astype(F32)).astype(BF16)


def eliminate(block_ref):
    count = B // 8
    sub = lax.broadcasted_iota(jnp.int32, (8, B), 0)
    lane = lax.broadcasted_iota(jnp.int32, (8, B), 1)
    a = [block_ref[8 * r : 8 * r + 8, :B] for r in range(count)]
    m = [jnp.where(lane == sub + 8 * r, 1.0, 0.0).astype(F32) for r in range(count)]
    scale = [jnp.ones((8, B), F32) for _ in range(count)]
    for j in range(B):
        p, jj = divmod(j, 8)
        column = jnp.broadcast_to(a[p][:, j : j + 1], (8, B))
        pivot = jnp.broadcast_to(column[jj : jj + 1, :], (8, B))
        inverse = 1.0 / pivot
        scale[p] = jnp.where(sub == jj, lax.rsqrt(pivot), scale[p])
        row_a = jnp.broadcast_to(a[p][jj : jj + 1, :], (8, B)) * inverse
        row_m = jnp.broadcast_to(m[p][jj : jj + 1, :], (8, B)) * inverse
        for r in range(p, count):
            if r == p:
                if jj == 7:
                    continue
                factor = jnp.where(sub > jj, column, 0.0)
            else:
                factor = jnp.broadcast_to(a[r][:, j : j + 1], (8, B))
            a[r] = a[r] - factor * row_a
            m[r] = m[r] - factor * row_m
    upper = [jnp.where(lane >= sub + 8 * r, a[r] * scale[r], 0.0) for r in range(count)]
    inv = [m[r] * scale[r] for r in range(count)]
    return jnp.concatenate(upper, 0), jnp.concatenate(inv, 0)


def step_kernel(k, rest, *refs):
    s_ref = refs[0]
    refs = refs[1:]
    t_ref = None
    if k:
        t_ref, refs = refs[0], refs[1:]
    l_ref, x_ref = refs[0], refs[1]
    upper, inv = eliminate(s_ref)
    l_ref[:B, :] = upper.T
    if k:
        x_ref[:, : B * k] = dot(inv, t_ref[:B, :])
    x_ref[:, B * k :] = inv
    if rest:
        panel = dot(s_ref[B:, :B], inv, ((1,), (1,)))
        l_ref[B:, :] = panel
        s_out, t_out = refs[2], refs[3]
        s_out[...] = s_ref[B:, B:] - dot(panel, panel, ((1,), (1,)))
        if k:
            t_out[:, : B * k] = t_ref[B:, :] - dot(panel, x_ref[:, : B * k])
        t_out[:, B * k :] = -dot(panel, inv)


def finish_kernel(nb, *refs):
    ls, xs, panel_ref = refs[:nb], refs[nb : 2 * nb], refs[2 * nb]
    l_ref, si_ref, f_ref, x_ref = refs[2 * nb + 1 :]
    l_ref[...] = jnp.zeros_like(l_ref)
    x_ref[...] = jnp.zeros_like(x_ref)
    for k in range(nb):
        l_ref[B * k :, B * k : B * k + B] = ls[k][...]
        x_ref[B * k : B * k + B, : B * k + B] = xs[k][...]
    x = x_ref[...]
    f_ref[...] = dot(panel_ref[...], x, ((1,), (1,)))
    si_ref[...] = dot(x, x, ((0,), (0,)))


def cost(flops, size):
    return pl.CostEstimate(flops=int(flops), bytes_accessed=int(size), transcendentals=0)


PARAMS = dict(vmem_limit_bytes=40 << 20)


def factorize(whole_diag, panel):
    size = whole_diag.shape[0]
    nb = size // B
    s, t = whole_diag, None
    ls, xs = [], []
    for k in range(nb):
        n = size - B * k
        rest = n - B
        out = [jax.ShapeDtypeStruct((n, B), F32), jax.ShapeDtypeStruct((B, B * (k + 1)), F32)]
        if rest:
            out += [jax.ShapeDtypeStruct((rest, rest), F32), jax.ShapeDtypeStruct((rest, B * (k + 1)), F32)]
        args = [s] + ([t] if k else [])
        res = pl.pallas_call(
            functools.partial(step_kernel, k, rest),
            out_shape=out,
            in_specs=[VMEM] * len(args),
            out_specs=[VMEM] * len(out),
            compiler_params=pltpu.CompilerParams(**PARAMS),
            cost_estimate=cost(14e9, 4 * n * n),
            name="diag_step",
        )(*args)
        ls.append(res[0])
        xs.append(res[1])
        if rest:
            s, t = res[2], res[3]
    return pl.pallas_call(
        functools.partial(finish_kernel, nb),
        out_shape=[
            jax.ShapeDtypeStruct((size, size), F32),
            jax.ShapeDtypeStruct((size, size), F32),
            jax.ShapeDtypeStruct(panel.shape, F32),
        ],
        in_specs=[VMEM] * (2 * nb + 1),
        out_specs=[VMEM] * 3,
        scratch_shapes=[pltpu.VMEM((size, size), F32)],
        compiler_params=pltpu.CompilerParams(**PARAMS),
        cost_estimate=cost(8e9, 4 * 5 * size * size),
        name="diag_finish",
    )(*ls, *xs, panel)


def update_kernel(si_ref, col_ref, row_ref, t_ref, o_ref, w_ref):
    k = si_ref.shape[0]

    @pl.when(pl.program_id(0) == 0)
    def _():
        high, low = split(si_ref[...])
        left = jnp.concatenate([high, high, low], 1)
        width = w_ref.shape[1]
        tile = 256 if width % 256 == 0 else width
        for c in range(0, width, tile):
            bh, bl = split(col_ref[c : c + tile, :])
            right = jnp.concatenate([bh, bl, bh], 1)
            w = dot(left, right, ((1,), (1,)), lax.Precision.DEFAULT)
            wh, wl = split(w)
            w_ref[:k, c : c + tile] = wh
            w_ref[k : 2 * k, c : c + tile] = wl
            w_ref[2 * k :, c : c + tile] = wh

    high, low = split(row_ref[...])
    a = jnp.concatenate([high, high, low], 1)
    o_ref[...] = t_ref[...] - dot(a, w_ref[...], precision=lax.Precision.DEFAULT)


def update(inverse, columns, rows, trailing):
    m, n = trailing.shape
    k = inverse.shape[0]
    tm = 256
    return pl.pallas_call(
        update_kernel,
        grid=(m // tm,),
        out_shape=jax.ShapeDtypeStruct((m, n), F32),
        in_specs=[
            VMEM,
            VMEM,
            pl.BlockSpec((tm, k), lambda i: (i, 0)),
            pl.BlockSpec((tm, n), lambda i: (i, 0)),
        ],
        out_specs=pl.BlockSpec((tm, n), lambda i: (i, 0)),
        scratch_shapes=[pltpu.VMEM((3 * k, n), BF16)],
        compiler_params=pltpu.CompilerParams(vmem_limit_bytes=58 << 20),
        cost_estimate=cost(6 * m * n * k, 8 * m * n),
        name="trailing_update",
    )(inverse, columns, rows, trailing)


def gather_diag(diag_block, n_row):
    rows = diag_block.shape[0]
    me = lax.axis_index("prow")
    whole = jnp.zeros((rows * n_row, diag_block.shape[1]), F32)
    whole = lax.dynamic_update_slice_in_dim(whole, diag_block, me * rows, 0)
    for d in range(1, n_row):
        got = lax.ppermute(diag_block, "prow", [(i, (i + d) % n_row) for i in range(n_row)])
        whole = lax.dynamic_update_slice_in_dim(whole, got, (me + n_row - d) % n_row * rows, 0)
    return whole


ORDER = (0, 2, 4, 6, 7, 5, 3, 1)


def gather_ring(panel, n_row, n_col):
    rows, width = panel.shape
    me, mine = lax.axis_index("prow"), lax.axis_index("pcol")
    place = {c: i for i, c in enumerate(ORDER)}
    right = [(ORDER[i], ORDER[(i + 1) % n_col]) for i in range(n_col)]
    left = [(b, a) for a, b in right]
    at = lambda o: jnp.asarray([ORDER[(place[c] + o) % n_col] for c in range(n_col)], jnp.int32)[mine]

    def put(buf, value, o, start=0):
        return lax.dynamic_update_slice_in_dim(buf, value, at(o) * rows + start, 0)

    owner_of = [c * n_row // n_col for c in range(n_col)]
    owner = mine * n_row // n_col
    need = []
    for c in range(n_col):
        first = c * n_row % n_col
        wanted = list(range(first, first + n_row))
        far = lambda w: min((place[w] - place[c]) % n_col, (place[c] - place[w]) % n_col)
        need.append(sorted(wanted, key=far))
    need = jnp.asarray(need, jnp.int32)
    axes = ("prow", "pcol")
    across = [(owner_of[c] * n_col + c, (owner_of[c] ^ 2) * n_col + c) for c in range(n_col)]
    beside = [(o * n_col + c, (o ^ 1) * n_col + c) for c in range(n_col) for o in (owner_of[c], owner_of[c] ^ 2)]
    column = jnp.zeros((rows * n_row, width), F32)

    def send_column(column, buf, slot):
        which = need[mine, slot]
        block = lax.dynamic_slice_in_dim(buf, which * rows, rows, 0)
        got = lax.ppermute(block, axes, across)
        block = jnp.where(me == owner, block, got)
        got = lax.ppermute(block, axes, beside)
        block = jnp.where((me == owner) | (me == (owner ^ 2)), block, got)
        return lax.dynamic_update_slice_in_dim(column, block, which % n_row * rows, 0)

    buf = jnp.zeros((rows * n_col, width), F32)
    buf = put(buf, panel, 0)
    from_left = from_right = panel
    for s in (1, 2, 3):
        from_left = lax.ppermute(from_left, "pcol", right)
        from_right = lax.ppermute(from_right, "pcol", left)
        buf = put(buf, from_left, -s)
        buf = put(buf, from_right, s)
        if s == 2:
            column = send_column(column, buf, 0)
        if s == 3:
            column = send_column(column, buf, 1)
            column = send_column(column, buf, 2)
    half = rows // 2
    low = lax.ppermute(from_left[:half], "pcol", right)
    high = lax.ppermute(from_right[half:], "pcol", left)
    buf = put(buf, low, 4)
    buf = put(buf, high, 4, half)
    column = send_column(column, buf, 3)
    return buf, column


def gather_plain(panel, n_row, n_col):
    rows = panel.shape[0]
    me, mine = lax.axis_index("prow"), lax.axis_index("pcol")
    row_panel = lax.all_gather(panel, "pcol", axis=0, tiled=True)
    owner = mine * n_row // n_col
    start = mine * n_row * rows - owner * n_col * rows
    block = lax.dynamic_slice_in_dim(row_panel, start, n_row * rows, 0)
    return row_panel, lax.psum(jnp.where(me == owner, block, 0.0), "prow")


def local(n_row, n_col, diag_block, panel_below, trailing):
    whole_diag = gather_diag(diag_block, n_row)
    gather = gather_ring if (n_row, n_col) == (4, 8) else gather_plain
    rows, columns = gather(panel_below, n_row, n_col)
    factor, inverse, own = factorize(whole_diag, panel_below)
    diag_rows = diag_block.shape[0]
    factor_diag = lax.dynamic_slice_in_dim(factor, lax.axis_index("prow") * diag_rows, diag_rows, 0)
    return factor_diag, own, update(inverse, columns, rows, trailing)


def solution(mesh):
    return jax.shard_map(
        functools.partial(local, mesh.shape["prow"], mesh.shape["pcol"]),
        mesh=mesh,
        in_specs=(P("prow", None), P(("prow", "pcol"), None), P("prow", "pcol")),
        out_specs=(P("prow", None), P(("prow", "pcol"), None), P("prow", "pcol")),
        check_vma=False,
    )
```

```python
import functools

import jax
import jax.numpy as jnp
import numpy as np
from jax import lax
from jax.experimental import pallas as pl
from jax.experimental.pallas import tpu as pltpu
from jax.sharding import PartitionSpec as P

B = 128
F32 = jnp.float32
BF16 = jnp.bfloat16
VMEM = pl.BlockSpec(memory_space=pltpu.VMEM)


def dot(a, b, contract=((1,), (0,)), precision=lax.Precision.HIGHEST):
    return lax.dot_general(a, b, (contract, ((), ())), precision=precision, preferred_element_type=F32)


def split(x):
    high = x.astype(BF16)
    return high, (x - high.astype(F32)).astype(BF16)


def eliminate(block_ref):
    count = B // 8
    sub = lax.broadcasted_iota(jnp.int32, (8, B), 0)
    lane = lax.broadcasted_iota(jnp.int32, (8, B), 1)
    a = [block_ref[8 * r : 8 * r + 8, :B] for r in range(count)]
    m = [jnp.where(lane == sub + 8 * r, 1.0, 0.0).astype(F32) for r in range(count)]
    scale = [jnp.ones((8, B), F32) for _ in range(count)]
    for j in range(0, B, 2):
        p, jj = divmod(j, 8)
        row = lambda x, i: jnp.broadcast_to(x[i : i + 1, :], (8, B))
        first = jnp.broadcast_to(a[p][:, j : j + 1], (8, B))
        second = jnp.broadcast_to(a[p][:, j + 1 : j + 2], (8, B))
        pivot, cross = row(first, jj), row(first, jj + 1)
        inverse = 1.0 / pivot
        ratio = cross * inverse
        pivot2 = row(second, jj + 1) - cross * ratio
        inverse2 = 1.0 / pivot2
        scale[p] = jnp.where(sub == jj, lax.rsqrt(pivot), scale[p])
        scale[p] = jnp.where(sub == jj + 1, lax.rsqrt(pivot2), scale[p])
        a1, m1 = row(a[p], jj), row(m[p], jj)
        a2 = (row(a[p], jj + 1) - ratio * a1) * inverse2
        m2 = (row(m[p], jj + 1) - ratio * m1) * inverse2
        a1, m1 = a1 * inverse, m1 * inverse
        for r in range(p, count):
            if r == p:
                f1 = jnp.where(sub > jj, first, 0.0)
                f2 = jnp.where(sub > jj + 1, second - first * ratio, 0.0)
            else:
                f1 = jnp.broadcast_to(a[r][:, j : j + 1], (8, B))
                f2 = jnp.broadcast_to(a[r][:, j + 1 : j + 2], (8, B)) - f1 * ratio
            a[r] = a[r] - f1 * a1 - f2 * a2
            m[r] = m[r] - f1 * m1 - f2 * m2
    upper = [jnp.where(lane >= sub + 8 * r, a[r] * scale[r], 0.0) for r in range(count)]
    inv = [m[r] * scale[r] for r in range(count)]
    return jnp.concatenate(upper, 0), jnp.concatenate(inv, 0)


def step_kernel(k, rest, pieces, *refs):
    t_ref = None
    if k:
        s_ref, t_ref, refs = refs[0], refs[1], refs[2:]
    else:
        places, parts, refs, s_ref = refs[0], refs[1 : 1 + pieces], refs[1 + pieces : -1], refs[-1]
        rows = parts[0].shape[0]
        for i, part in enumerate(parts):
            s_ref[pl.ds(pl.multiple_of(places[i] * rows, 8), rows), :] = part[...]
    l_ref, x_ref = refs[0], refs[1]
    upper, inv = eliminate(s_ref)
    l_ref[:B, :] = upper.T
    if k:
        x_ref[:, : B * k] = dot(inv, t_ref[:B, :])
    x_ref[:, B * k :] = inv
    if rest:
        panel = dot(s_ref[B:, :B], inv, ((1,), (1,)))
        l_ref[B:, :] = panel
        s_out, t_out = refs[2], refs[3]
        s_out[...] = s_ref[B:, B:] - dot(panel, panel, ((1,), (1,)))
        if k:
            t_out[:, : B * k] = t_ref[B:, :] - dot(panel, x_ref[:, : B * k])
        t_out[:, B * k :] = -dot(panel, inv)


def finish_kernel(nb, *refs):
    ls, xs, panel_ref = refs[:nb], refs[nb : 2 * nb], refs[2 * nb]
    l_ref, si_ref, f_ref, x_ref = refs[2 * nb + 1 :]
    l_ref[...] = jnp.zeros_like(l_ref)
    x_ref[...] = jnp.zeros_like(x_ref)
    for k in range(nb):
        l_ref[B * k :, B * k : B * k + B] = ls[k][...]
        x_ref[B * k : B * k + B, : B * k + B] = xs[k][...]
    x = x_ref[...]
    f_ref[...] = dot(panel_ref[...], x, ((1,), (1,)))
    si_ref[...] = dot(x, x, ((0,), (0,)))


def cost(flops, size):
    return pl.CostEstimate(flops=int(flops), bytes_accessed=int(size), transcendentals=0)


PARAMS = dict(vmem_limit_bytes=40 << 20)


def factorize(parts, places, panel):
    size = parts[0].shape[1]
    nb = size // B
    s = t = None
    ls, xs = [], []
    for k in range(nb):
        n = size - B * k
        rest = n - B
        out = [jax.ShapeDtypeStruct((n, B), F32), jax.ShapeDtypeStruct((B, B * (k + 1)), F32)]
        if rest:
            out += [jax.ShapeDtypeStruct((rest, rest), F32), jax.ShapeDtypeStruct((rest, B * (k + 1)), F32)]
        args = [s, t] if k else [places, *parts]
        specs = [VMEM] * len(args)
        if not k:
            specs[0] = pl.BlockSpec(memory_space=pltpu.SMEM)
        res = pl.pallas_call(
            functools.partial(step_kernel, k, rest, len(parts)),
            out_shape=out,
            in_specs=specs,
            out_specs=[VMEM] * len(out),
            scratch_shapes=[] if k else [pltpu.VMEM((size, size), F32)],
            compiler_params=pltpu.CompilerParams(**PARAMS),
            cost_estimate=cost(12e9, 4 * n * n),
            name="diag_step",
        )(*args)
        ls.append(res[0])
        xs.append(res[1])
        if rest:
            s, t = res[2], res[3]
    return pl.pallas_call(
        functools.partial(finish_kernel, nb),
        out_shape=[
            jax.ShapeDtypeStruct((size, size), F32),
            jax.ShapeDtypeStruct((size, size), F32),
            jax.ShapeDtypeStruct(panel.shape, F32),
        ],
        in_specs=[VMEM] * (2 * nb + 1),
        out_specs=[VMEM] * 3,
        scratch_shapes=[pltpu.VMEM((size, size), F32)],
        compiler_params=pltpu.CompilerParams(**PARAMS),
        cost_estimate=cost(8e9, 4 * 5 * size * size),
        name="diag_finish",
    )(*ls, *xs, panel)


def update_kernel(pieces, tiles, parts, has_old, index_ref, si_ref, *refs):
    cols, rows, refs = refs[:parts], refs[parts : parts + pieces], refs[parts + pieces :]
    t_ref = refs[0]
    o_ref, w_ref, a_ref, c_ref = refs[2:] if has_old else refs[1:]
    k = si_ref.shape[0]
    step = pl.program_id(0)

    @pl.when(step == 0)
    def _():
        high, low = split(si_ref[...])
        left = jnp.concatenate([high, high, low], 1)
        height = cols[0].shape[0]
        for i, col in enumerate(cols):
            c_ref[pl.ds(pl.multiple_of(index_ref[pieces + 1 + i] * height, 8), height), :] = col[...]
        width = w_ref.shape[1]
        tile = 384 if width % 384 == 0 else width
        for c in range(0, width, tile):
            bh, bl = split(c_ref[c : c + tile, :])
            right = jnp.concatenate([bh, bl, bh], 1)
            w = dot(left, right, ((1,), (1,)), lax.Precision.DEFAULT)
            wh, wl = split(w)
            w_ref[:k, c : c + tile] = wh
            w_ref[k : 2 * k, c : c + tile] = wl
            w_ref[2 * k :, c : c + tile] = wh

    for b in range(pieces):

        @pl.when(step // tiles == b)
        def _():
            high, low = split(rows[b][...])
            a_ref[:, :k] = high
            a_ref[:, k : 2 * k] = high
            a_ref[:, 2 * k :] = low

    o_ref[...] = t_ref[...] - dot(a_ref[...], w_ref[...], precision=lax.Precision.DEFAULT)


def update(inverse, columns, rows, index, trailing, old=None):
    m, n = trailing.shape
    k = inverse.shape[0]
    pieces, parts = len(rows), len(columns)
    width = parts * columns[0].shape[0]
    tm = 288
    tiles = rows[0].shape[0] // tm

    def piece_map(b):
        return lambda i, index: (jnp.clip(i - b * tiles, 0, tiles - 1), 0)

    def out_map(i, index):
        return index[i // tiles] * tiles + i % tiles, index[pieces]

    args = [inverse, *columns, *rows, trailing]
    specs = [VMEM] * (1 + parts)
    specs += [pl.BlockSpec((tm, k), piece_map(b)) for b in range(pieces)]
    specs += [pl.BlockSpec((tm, width), out_map)]
    if old is not None:
        args.append(old)
        specs.append(pl.BlockSpec(memory_space=pl.ANY))
    return pl.pallas_call(
        functools.partial(update_kernel, pieces, tiles, parts, old is not None),
        grid_spec=pltpu.PrefetchScalarGridSpec(
            num_scalar_prefetch=1,
            grid=(m // tm,),
            in_specs=specs,
            out_specs=pl.BlockSpec((tm, width), out_map),
            scratch_shapes=[
                pltpu.VMEM((3 * k, width), BF16),
                pltpu.VMEM((tm, 3 * k), BF16),
                pltpu.VMEM((width, k), F32),
            ],
        ),
        out_shape=jax.ShapeDtypeStruct((m, n), F32),
        input_output_aliases={len(args): 0} if old is not None else {},
        compiler_params=pltpu.CompilerParams(vmem_limit_bytes=56 << 20),
        cost_estimate=cost(6 * m * width * k, 8 * m * width),
        name="trailing_update",
    )(index, *args)


ORDER = (0, 2, 4, 6, 7, 5, 3, 1)
OFFSETS = (0, -1, 1, -2, 2, -3, 3, 4)


def ring_tables(n_row, n_col):
    place = {c: i for i, c in enumerate(ORDER)}
    index, chosen, role = [], [], []
    for r in range(n_row):
        for c in range(n_col):
            at = lambda o: ORDER[(place[c] + o) % n_col]
            seen = {at(o): i for i, o in enumerate(OFFSETS)}
            first = c * n_row % n_col
            pairs = [[first, first + 1], [first + 2, first + 3]]
            reach = lambda w: (seen[w] + 1) // 2
            pairs = [sorted(pair, key=lambda w: seen[w]) for pair in pairs]
            pairs.sort(key=lambda pair: reach(pair[1]))
            rows = [at(o) for o in OFFSETS]
            index.append([rows + [(pair[0] - first) // 2] + [w % 2 for w in pair] for pair in pairs])
            chosen.append([seen[w] for pair in pairs for w in pair])
            owner = c * n_row // n_col
            role.append(0 if r == owner else 1 if r == owner ^ 2 else 2)
    return np.asarray(index, np.int32), np.asarray(chosen, np.int32), np.asarray(role, np.int32)


def gather_ring(panel, n_row, n_col):
    rows = panel.shape[0]
    me = lax.axis_index("prow") * n_col + lax.axis_index("pcol")
    index, chosen, role = ring_tables(n_row, n_col)
    flat = np.concatenate([index.reshape(len(role), -1), chosen, role[:, None]], 1)
    mine = lax.dynamic_slice_in_dim(jnp.asarray(flat), me, 1, 0)[0]
    size = index.shape[2]
    tables = [mine[:size], mine[size : 2 * size]]
    choice, own_role = mine[2 * size : 2 * size + 4], mine[-1]
    right = [(ORDER[i], ORDER[(i + 1) % n_col]) for i in range(n_col)]
    left = [(b, a) for a, b in right]
    owner_of = [c * n_row // n_col for c in range(n_col)]
    axes = ("prow", "pcol")
    across = [(owner_of[c] * n_col + c, (owner_of[c] ^ 2) * n_col + c) for c in range(n_col)]
    beside = [(o * n_col + c, (o ^ 1) * n_col + c) for c in range(n_col) for o in (owner_of[c], owner_of[c] ^ 2)]

    def send_column(held, slot):
        used = sorted(set(chosen[:, slot].tolist()))
        block = held[used[0]]
        for u in used[1:]:
            block = jnp.where(choice[slot] == u, held[u], block)
        got = lax.ppermute(block, axes, across)
        block = jnp.where(own_role == 0, block, got)
        got = lax.ppermute(block, axes, beside)
        return jnp.where(own_role == 2, got, block)

    held = [panel]
    from_left = from_right = panel
    slots = []
    for s in (1, 2, 3):
        from_left = lax.ppermute(from_left, "pcol", right)
        from_right = lax.ppermute(from_right, "pcol", left)
        held += [from_left, from_right]
        if s == 2:
            slots.append(send_column(held, 0))
        if s == 3:
            slots += [send_column(held, 1), send_column(held, 2)]
    half = rows // 2
    low = lax.ppermute(from_left[:half], "pcol", right)
    high = lax.ppermute(from_right[half:], "pcol", left)
    held.append(jnp.concatenate([low, high], 0))
    slots.append(send_column(held, 3))
    return held, [(slots[:2], tables[0]), (slots[2:], tables[1])]


def gather_plain(panel, n_row, n_col):
    rows = panel.shape[0]
    me, mine = lax.axis_index("prow"), lax.axis_index("pcol")
    row_panel = lax.all_gather(panel, "pcol", axis=0, tiled=True)
    owner = mine * n_row // n_col
    start = mine * n_row * rows - owner * n_col * rows
    block = lax.dynamic_slice_in_dim(row_panel, start, n_row * rows, 0)
    column = lax.psum(jnp.where(me == owner, block, 0.0), "prow")
    return [row_panel], [([column], jnp.zeros((3,), jnp.int32))]


def local(n_row, n_col, diag_block, panel_below, trailing):
    me = lax.axis_index("prow")
    shift = lambda d: [(i, (i + d) % n_row) for i in range(n_row)]
    parts = [diag_block] + [lax.ppermute(diag_block, "prow", shift(d)) for d in range(1, n_row)]
    places = lax.rem(me + n_row - jnp.arange(n_row, dtype=jnp.int32), n_row)
    gather = gather_ring if (n_row, n_col) == (4, 8) else gather_plain
    rows, columns = gather(panel_below, n_row, n_col)
    factor, inverse, own = factorize(parts, places, panel_below)
    diag_rows = diag_block.shape[0]
    factor_diag = lax.dynamic_slice_in_dim(factor, me * diag_rows, diag_rows, 0)
    updated = None
    for block, index in columns:
        updated = update(inverse, block, rows, index, trailing, updated)
    return factor_diag, own, updated


def solution(mesh):
    return jax.shard_map(
        functools.partial(local, mesh.shape["prow"], mesh.shape["pcol"]),
        mesh=mesh,
        in_specs=(P("prow", None), P(("prow", "pcol"), None), P("prow", "pcol")),
        out_specs=(P("prow", None), P(("prow", "pcol"), None), P("prow", "pcol")),
        check_vma=False,
    )
```

```python
import functools

import jax
import jax.numpy as jnp
import numpy as np
from jax import lax
from jax.experimental import pallas as pl
from jax.experimental.pallas import tpu as pltpu
from jax.sharding import PartitionSpec as P

B = 128
F32 = jnp.float32
BF16 = jnp.bfloat16
VMEM = pl.BlockSpec(memory_space=pltpu.VMEM)


def dot(a, b, contract=((1,), (0,)), precision=lax.Precision.HIGHEST):
    return lax.dot_general(a, b, (contract, ((), ())), precision=precision, preferred_element_type=F32)


def split(x):
    high = x.astype(BF16)
    return high, (x - high.astype(F32)).astype(BF16)


def eliminate(block_ref):
    count = B // 8
    sub = lax.broadcasted_iota(jnp.int32, (8, B), 0)
    lane = lax.broadcasted_iota(jnp.int32, (8, B), 1)
    a = [block_ref[8 * r : 8 * r + 8, :B] for r in range(count)]
    m = [jnp.where(lane == sub + 8 * r, 1.0, 0.0).astype(F32) for r in range(count)]
    scale = [jnp.ones((8, B), F32) for _ in range(count)]
    for j in range(0, B, 2):
        p, jj = divmod(j, 8)
        row = lambda x, i: jnp.broadcast_to(x[i : i + 1, :], (8, B))
        first = jnp.broadcast_to(a[p][:, j : j + 1], (8, B))
        second = jnp.broadcast_to(a[p][:, j + 1 : j + 2], (8, B))
        pivot, cross = row(first, jj), row(first, jj + 1)
        inverse = 1.0 / pivot
        ratio = cross * inverse
        pivot2 = row(second, jj + 1) - cross * ratio
        inverse2 = 1.0 / pivot2
        scale[p] = jnp.where(sub == jj, lax.rsqrt(pivot), scale[p])
        scale[p] = jnp.where(sub == jj + 1, lax.rsqrt(pivot2), scale[p])
        a1, m1 = row(a[p], jj), row(m[p], jj)
        a2 = (row(a[p], jj + 1) - ratio * a1) * inverse2
        m2 = (row(m[p], jj + 1) - ratio * m1) * inverse2
        a1, m1 = a1 * inverse, m1 * inverse
        for r in range(p, count):
            if r == p:
                f1 = jnp.where(sub > jj, first, 0.0)
                f2 = jnp.where(sub > jj + 1, second - first * ratio, 0.0)
            else:
                f1 = jnp.broadcast_to(a[r][:, j : j + 1], (8, B))
                f2 = jnp.broadcast_to(a[r][:, j + 1 : j + 2], (8, B)) - f1 * ratio
            a[r] = a[r] - f1 * a1 - f2 * a2
            m[r] = m[r] - f1 * m1 - f2 * m2
    upper = [jnp.where(lane >= sub + 8 * r, a[r] * scale[r], 0.0) for r in range(count)]
    inv = [m[r] * scale[r] for r in range(count)]
    return jnp.concatenate(upper, 0), jnp.concatenate(inv, 0)


def step_kernel(k, rest, pieces, *refs):
    t_ref = None
    if k:
        s_ref, t_ref, refs = refs[0], refs[1], refs[2:]
    else:
        places, parts, refs, s_ref = refs[0], refs[1 : 1 + pieces], refs[1 + pieces : -1], refs[-1]
        rows = parts[0].shape[0]
        for i, part in enumerate(parts):
            s_ref[pl.ds(pl.multiple_of(places[i] * rows, 8), rows), :] = part[...]
    l_ref, x_ref = refs[0], refs[1]
    upper, inv = eliminate(s_ref)
    l_ref[:B, :] = upper.T
    if k:
        x_ref[:, : B * k] = dot(inv, t_ref[:B, :])
    x_ref[:, B * k :] = inv
    if rest:
        panel = dot(s_ref[B:, :B], inv, ((1,), (1,)))
        l_ref[B:, :] = panel
        s_out, t_out = refs[2], refs[3]
        s_out[...] = s_ref[B:, B:] - dot(panel, panel, ((1,), (1,)))
        if k:
            t_out[:, : B * k] = t_ref[B:, :] - dot(panel, x_ref[:, : B * k])
        t_out[:, B * k :] = -dot(panel, inv)


def finish_kernel(nb, *refs):
    ls, xs, panel_ref = refs[:nb], refs[nb : 2 * nb], refs[2 * nb]
    l_ref, si_ref, f_ref, x_ref = refs[2 * nb + 1 :]
    l_ref[...] = jnp.zeros_like(l_ref)
    x_ref[...] = jnp.zeros_like(x_ref)
    for k in range(nb):
        l_ref[B * k :, B * k : B * k + B] = ls[k][...]
        x_ref[B * k : B * k + B, : B * k + B] = xs[k][...]
    x = x_ref[...]
    f_ref[...] = dot(panel_ref[...], x, ((1,), (1,)))
    si_ref[...] = dot(x, x, ((0,), (0,)))


def cost(flops, size):
    return pl.CostEstimate(flops=int(flops), bytes_accessed=int(size), transcendentals=0)


PARAMS = dict(vmem_limit_bytes=40 << 20)


def factorize(parts, places, panel):
    size = parts[0].shape[1]
    nb = size // B
    s = t = None
    ls, xs = [], []
    for k in range(nb):
        n = size - B * k
        rest = n - B
        out = [jax.ShapeDtypeStruct((n, B), F32), jax.ShapeDtypeStruct((B, B * (k + 1)), F32)]
        if rest:
            out += [jax.ShapeDtypeStruct((rest, rest), F32), jax.ShapeDtypeStruct((rest, B * (k + 1)), F32)]
        args = [s, t] if k else [places, *parts]
        specs = [VMEM] * len(args)
        if not k:
            specs[0] = pl.BlockSpec(memory_space=pltpu.SMEM)
        res = pl.pallas_call(
            functools.partial(step_kernel, k, rest, len(parts)),
            out_shape=out,
            in_specs=specs,
            out_specs=[VMEM] * len(out),
            scratch_shapes=[] if k else [pltpu.VMEM((size, size), F32)],
            compiler_params=pltpu.CompilerParams(**PARAMS),
            cost_estimate=cost(12e9, 4 * n * n),
            name="diag_step",
        )(*args)
        ls.append(res[0])
        xs.append(res[1])
        if rest:
            s, t = res[2], res[3]
    outs = pl.pallas_call(
        functools.partial(finish_kernel, nb),
        out_shape=[
            jax.ShapeDtypeStruct((size, size), F32),
            jax.ShapeDtypeStruct((size, size), F32),
            jax.ShapeDtypeStruct(panel.shape, F32),
        ],
        in_specs=[VMEM] * (2 * nb + 1),
        out_specs=[VMEM] * 3,
        scratch_shapes=[pltpu.VMEM((size, size), F32)],
        compiler_params=pltpu.CompilerParams(**PARAMS),
        cost_estimate=cost(8e9, 4 * 5 * size * size),
        name="diag_finish",
    )(*ls, *xs, panel)
    return *outs, xs


def update_kernel(pieces, tiles, parts, has_old, index_ref, si_ref, *refs):
    cols, rows, refs = refs[:parts], refs[parts : parts + pieces], refs[parts + pieces :]
    t_ref = refs[0]
    o_ref, w_ref, a_ref, c_ref = refs[2:] if has_old else refs[1:]
    k = si_ref.shape[0]
    step = pl.program_id(0)

    @pl.when(step == 0)
    def _():
        high, low = split(si_ref[...])
        left = jnp.concatenate([high, high, low], 1)
        height = cols[0].shape[0]
        for i, col in enumerate(cols):
            c_ref[pl.ds(pl.multiple_of(index_ref[pieces + 1 + i] * height, 8), height), :] = col[...]
        width = w_ref.shape[1]
        tile = 384 if width % 384 == 0 else width
        for c in range(0, width, tile):
            bh, bl = split(c_ref[c : c + tile, :])
            right = jnp.concatenate([bh, bl, bh], 1)
            w = dot(left, right, ((1,), (1,)), lax.Precision.DEFAULT)
            wh, wl = split(w)
            w_ref[:k, c : c + tile] = wh
            w_ref[k : 2 * k, c : c + tile] = wl
            w_ref[2 * k :, c : c + tile] = wh

    for b in range(pieces):

        @pl.when(step // tiles == b)
        def _():
            high, low = split(rows[b][...])
            a_ref[:, :k] = high
            a_ref[:, k : 2 * k] = high
            a_ref[:, 2 * k :] = low

    o_ref[...] = t_ref[...] - dot(a_ref[...], w_ref[...], precision=lax.Precision.DEFAULT)


def update(inverse, columns, rows, index, trailing, old=None):
    m, n = trailing.shape
    k = inverse.shape[0]
    pieces, parts = len(rows), len(columns)
    width = parts * columns[0].shape[0]
    tm = 288
    tiles = rows[0].shape[0] // tm

    def piece_map(b):
        return lambda i, index: (jnp.clip(i - b * tiles, 0, tiles - 1), 0)

    def out_map(i, index):
        return index[i // tiles] * tiles + i % tiles, index[pieces]

    args = [inverse, *columns, *rows, trailing]
    specs = [VMEM] * (1 + parts)
    specs += [pl.BlockSpec((tm, k), piece_map(b)) for b in range(pieces)]
    specs += [pl.BlockSpec((tm, width), out_map)]
    if old is not None:
        args.append(old)
        specs.append(pl.BlockSpec(memory_space=pl.ANY))
    return pl.pallas_call(
        functools.partial(update_kernel, pieces, tiles, parts, old is not None),
        grid_spec=pltpu.PrefetchScalarGridSpec(
            num_scalar_prefetch=1,
            grid=(m // tm,),
            in_specs=specs,
            out_specs=pl.BlockSpec((tm, width), out_map),
            scratch_shapes=[
                pltpu.VMEM((3 * k, width), BF16),
                pltpu.VMEM((tm, 3 * k), BF16),
                pltpu.VMEM((width, k), F32),
            ],
        ),
        out_shape=jax.ShapeDtypeStruct((m, n), F32),
        input_output_aliases={len(args): 0} if old is not None else {},
        compiler_params=pltpu.CompilerParams(vmem_limit_bytes=56 << 20),
        cost_estimate=cost(6 * m * width * k, 8 * m * width),
        name="trailing_update",
    )(index, *args)


ORDER = (0, 2, 4, 6, 7, 5, 3, 1)
OFFSETS = (0, -1, 1, -2, 2, -3, 3, 4)


def ring_tables(n_row, n_col):
    place = {c: i for i, c in enumerate(ORDER)}
    index, chosen, role = [], [], []
    for r in range(n_row):
        for c in range(n_col):
            at = lambda o: ORDER[(place[c] + o) % n_col]
            seen = {at(o): i for i, o in enumerate(OFFSETS)}
            first = c * n_row % n_col
            pairs = [[first, first + 1], [first + 2, first + 3]]
            reach = lambda w: (seen[w] + 1) // 2
            pairs = [sorted(pair, key=lambda w: seen[w]) for pair in pairs]
            pairs.sort(key=lambda pair: reach(pair[1]))
            rows = [at(o) for o in OFFSETS]
            index.append([rows + [0] + [w - first for pair in pairs for w in pair]])
            chosen.append([seen[w] for pair in pairs for w in pair])
            owner = c * n_row // n_col
            role.append(0 if r == owner else 1 if r == owner ^ 2 else 2)
    return np.asarray(index, np.int32), np.asarray(chosen, np.int32), np.asarray(role, np.int32)


def gather_ring(panel, n_row, n_col, marks):
    rows = panel.shape[0]
    me = lax.axis_index("prow") * n_col + lax.axis_index("pcol")
    index, chosen, role = ring_tables(n_row, n_col)
    flat = np.concatenate([index.reshape(len(role), -1), chosen, role[:, None]], 1)
    mine = lax.dynamic_slice_in_dim(jnp.asarray(flat), me, 1, 0)[0]
    size = index.shape[2]
    choice, own_role = mine[size : size + 4], mine[-1]
    right = [(ORDER[i], ORDER[(i + 1) % n_col]) for i in range(n_col)]
    left = [(b, a) for a, b in right]
    owner_of = [c * n_row // n_col for c in range(n_col)]
    axes = ("prow", "pcol")
    across = [(owner_of[c] * n_col + c, (owner_of[c] ^ 2) * n_col + c) for c in range(n_col)]
    beside = [(o * n_col + c, (o ^ 1) * n_col + c) for c in range(n_col) for o in (owner_of[c], owner_of[c] ^ 2)]

    def send_column(held, slot):
        used = sorted(set(chosen[:, slot].tolist()))
        block = held[used[0]]
        for u in used[1:]:
            block = jnp.where(choice[slot] == u, held[u], block)
        got = lax.ppermute(block, axes, across)
        block = jnp.where(own_role == 0, block, got)
        got = lax.ppermute(block, axes, beside)
        return jnp.where(own_role == 2, got, block)

    held = [panel]
    from_left = from_right = panel
    slots = []
    for s in (1, 2, 3):
        if s > 1:
            from_left, from_right, _ = lax.optimization_barrier((from_left, from_right, marks[1 if s == 2 else -1]))
            held[-2:] = [from_left, from_right]
        from_left = lax.ppermute(from_left, "pcol", right)
        from_right = lax.ppermute(from_right, "pcol", left)
        held += [from_left, from_right]
        if s == 2:
            slots.append(send_column(held, 0))
        if s == 3:
            slots += [send_column(held, 1), send_column(held, 2)]
    from_left, from_right, slots[0] = lax.optimization_barrier((from_left, from_right, slots[0]))
    held[-2:] = [from_left, from_right]
    half = rows // 2
    low = lax.ppermute(from_left[:half], "pcol", right)
    high = lax.ppermute(from_right[half:], "pcol", left)
    held.append(jnp.concatenate([low, high], 0))
    slots.append(send_column(held, 3))
    return held, [(slots, mine[:size])]


def gather_plain(panel, n_row, n_col, marks):
    rows = panel.shape[0]
    me, mine = lax.axis_index("prow"), lax.axis_index("pcol")
    row_panel = lax.all_gather(panel, "pcol", axis=0, tiled=True)
    owner = mine * n_row // n_col
    start = mine * n_row * rows - owner * n_col * rows
    block = lax.dynamic_slice_in_dim(row_panel, start, n_row * rows, 0)
    column = lax.psum(jnp.where(me == owner, block, 0.0), "prow")
    return [row_panel], [([column], jnp.zeros((3,), jnp.int32))]


def local(n_row, n_col, diag_block, panel_below, trailing):
    me = lax.axis_index("prow")
    shift = lambda d: [(i, (i + d) % n_row) for i in range(n_row)]
    parts = [diag_block] + [lax.ppermute(diag_block, "prow", shift(d)) for d in range(1, n_row)]
    places = lax.rem(me + n_row - jnp.arange(n_row, dtype=jnp.int32), n_row)
    gather = gather_ring if (n_row, n_col) == (4, 8) else gather_plain
    factor, inverse, own, marks = factorize(parts, places, panel_below)
    rows, columns = gather(panel_below, n_row, n_col, marks)
    diag_rows = diag_block.shape[0]
    factor_diag = lax.dynamic_slice_in_dim(factor, me * diag_rows, diag_rows, 0)
    updated = None
    for block, index in columns:
        updated = update(inverse, block, rows, index, trailing, updated)
    return factor_diag, own, updated


def solution(mesh):
    return jax.shard_map(
        functools.partial(local, mesh.shape["prow"], mesh.shape["pcol"]),
        mesh=mesh,
        in_specs=(P("prow", None), P(("prow", "pcol"), None), P("prow", "pcol")),
        out_specs=(P("prow", None), P(("prow", "pcol"), None), P("prow", "pcol")),
        check_vma=False,
    )
```
